1024 devices in a mesh: graph: 256 (over z, y, core), group: 4 (over x).
Axes of the slice: x: 4, y: 4, z: 32, core: 2. Of those that a mesh axis runs over, the one named last changes fastest.
Arguments:
- state: bfloat16 [14, 1048576], P(None, 'graph'), may hold values from -6 to 6
- cotangent: float32 [4, 14, 1048576], P('group', None, 'graph'), may hold values from -6 to 6
- diffusivity: float32 [3, 2048], P(None, 'graph'), may hold values from 0.0001 to 0.001
- shared_nodes: int32 [256, 8, 384], P('graph'), may hold values from -1 to 4095, as said below
- w_in: bfloat16 [14, 128], replicated, may hold values from -1.5 to 1.5
- b_in: float32 [128], replicated, may hold values from -3 to 3
- w_mid: bfloat16 [128, 128], replicated, may hold values from -0.5 to 0.5
- b_mid: float32 [128], replicated, may hold values from -3 to 3
- w_out: bfloat16 [128, 14], replicated, may hold values from -0.5 to 0.5
Outputs:
- grad_state: float32 [4, 14, 1048576], P('group', None, 'graph')
- grad_w_in: float32 [14, 128], replicated
- grad_w_mid: float32 [128, 128], replicated
- grad_w_out: float32 [128, 14], replicated
The draws below stay inside these ranges and needn't reach their ends.
Inputs may be any that keep to these rules, and one draw needn't show every extreme that they name: `shared_nodes`: each partition-local node stands in at most one list of its partition; the lists of directions that leave the grid of 4 x (64) partitions are empty; every other list holds its nodes in its leading slots, matching its partner list's count: 192 to 384 nodes for the four face directions (o = +-1, +-4), with some list holding 384, and 24 to 48 nodes for the four diagonal directions, with some list holding 384 / 8.
All inputs are finite; a program needn't handle non-finite values.
Results may differ from the reference program's by a relative error of at most 0.0077.
Values sent between devices are 32-bit elements; how exact they have to be, the bound alone decides.
A program may use at most 32 MiB of HBM per device.

```python
import math
import jax
import jax.numpy as jnp
import numpy as np
from jax import lax

FIELDS = 14
HIDDEN_SIZE = 128
NODES = 512
PROWS = 4
E_DEV = 8
S_MAX = 384
PARTS_SIZE = 256
ELEMS = 2048
POINTS = 1048576
OBJECTIVES = 4


def shuffle_nodes(node_key):
    return jax.random.permutation(node_key, E_DEV * NODES)


def draw_shared_nodes(key, part):
    count_key, edge_key, pick_key, order_key = jax.random.split(key, 4)
    ranks = jnp.arange(PARTS_SIZE)
    across = ranks % PROWS
    column = ranks // PROWS
    last_column = PARTS_SIZE // PROWS - 1
    faces = jax.random.randint(count_key, (PARTS_SIZE, 2), S_MAX // 2, S_MAX + 1)
    edges = jax.random.randint(edge_key, (PARTS_SIZE, 2), S_MAX // 16, S_MAX // 8 + 1)
    forward = jnp.concatenate([faces, edges], axis=1)
    face_key, column_key, row_key = jax.random.split(pick_key, 3)
    chosen = jax.random.randint(face_key, (), 0, PARTS_SIZE - PROWS)
    forward = forward.at[chosen, 1].set(S_MAX)
    edge_column = jax.random.randint(column_key, (), 0, last_column)
    edge_row = jax.random.randint(row_key, (), 0, PROWS - 1)
    forward = forward.at[edge_column * PROWS + edge_row, 2].set(S_MAX // 8)
    linked = jnp.stack([across < PROWS - 1, column < last_column, (across < PROWS - 1) & (column < last_column), (across > 0) & (column < last_column)], axis=1)
    forward = jnp.where(linked, forward, 0)
    strides = [1, PROWS, PROWS + 1, PROWS - 1]
    columns = []
    for which, stride in enumerate(strides):
        columns.append(forward[:, which])
        columns.append(jnp.where(ranks >= stride, jnp.roll(forward[:, which], stride), 0))
    counts = jnp.stack(columns, axis=1)
    order_keys = jax.random.split(order_key, PARTS_SIZE)
    orders = jax.vmap(shuffle_nodes)(order_keys).astype(jnp.int32)
    lists = orders[:, :8 * S_MAX].reshape(PARTS_SIZE, 8, S_MAX)
    places = jnp.arange(S_MAX)
    return jnp.where(places[None, None, :] < counts[:, :, None], lists, -1).astype(jnp.int32)


def shard_levels(stream_key, shape, cuts, low, top_value):
    loudness, own = 1.0, jax.random.fold_in(stream_key, 6)
    for dim, parts in cuts:
        draws = jnp.exp(jax.random.uniform(jax.random.fold_in(own, dim), (parts,), jnp.float32, low / len(cuts), top_value / len(cuts)))
        loudness = loudness * jnp.repeat(draws, shape[dim] // parts).reshape([-1 if axis == dim else 1 for axis in range(len(shape))])
    return loudness


def scatter_about(key, shape, deviation, most, cuts=(), kind=jnp.bfloat16):
    entries = jax.random.normal(key, shape, jnp.float32) * deviation
    if len(cuts) > 0:
        entries = shard_levels(key, shape, cuts, -0.22, 0.18) * entries
    return jnp.clip(entries, min=-most, max=most).astype(kind)


def setup_inputs(seed: int = 0) -> dict:
    arg_keys = jax.random.split(jax.random.key(seed), 10)
    return {
        "state": scatter_about(arg_keys[0], (FIELDS, POINTS), 1.0, 6.0, ((1, 256),)),
        "cotangent": scatter_about(arg_keys[1], (OBJECTIVES, FIELDS, POINTS), 1.0, 6.0, ((0, 4), (2, 256)), jnp.float32),
        "diffusivity": jnp.clip(jnp.exp(math.log(0.001) - 2.3025852 * jax.random.uniform(arg_keys[2], (3, ELEMS), jnp.float32) ** shard_levels(arg_keys[2], (3, ELEMS), ((1, 256),), -0.2, 0.2)), 0.0001, 0.001),
        "shared_nodes": draw_shared_nodes(jax.random.fold_in(arg_keys[9], 71), 0),
        "w_in": scatter_about(arg_keys[4], (FIELDS, HIDDEN_SIZE), FIELDS ** -0.5, 1.5),
        "b_in": scatter_about(arg_keys[5], (HIDDEN_SIZE,), 0.5, 3.0, (), jnp.float32),
        "w_mid": scatter_about(arg_keys[6], (HIDDEN_SIZE, HIDDEN_SIZE), HIDDEN_SIZE ** -0.5, 0.5),
        "b_mid": scatter_about(arg_keys[7], (HIDDEN_SIZE,), 0.5, 3.0, (), jnp.float32),
        "w_out": scatter_about(arg_keys[8], (HIDDEN_SIZE, FIELDS), HIDDEN_SIZE ** -0.5, 0.5),
    }


step_scale = 0.5


def stiffness():
    order = 7
    points = np.cos(np.pi * np.arange(order + 1) / order)
    ends = np.ones(order + 1)
    ends[0] = 2.0
    ends[-1] = 2.0
    deriv = np.zeros((order + 1, order + 1))
    for first in range(order + 1):
        for second in range(order + 1):
            if first != second:
                deriv[first, second] = ends[first] / ends[second] * (-1.0) ** (first + second) / (points[first] - points[second])
    row_sums = deriv.sum(axis=1)
    for place in range(order + 1):
        deriv[place, place] = -row_sums[place]
    return jnp.asarray(deriv.T @ deriv, dtype=jnp.float32)


def peer_offsets():
    return [1, -1, PROWS, -PROWS, PROWS + 1, -PROWS - 1, PROWS - 1, -PROWS + 1]


def diffuse(blocks, diffusivity):
    table = stiffness()
    highest = lax.Precision.HIGHEST
    along_one = jnp.einsum('ab,lebjk->leajk', table, blocks, precision=highest)
    along_two = jnp.einsum('ab,leibk->leiak', table, blocks, precision=highest)
    along_three = jnp.einsum('ab,leijb->leija', table, blocks, precision=highest)
    coeff = [diffusivity[which][None, :, None, None, None] for which in range(3)]
    return -(coeff[0] * along_one + coeff[1] * along_two + coeff[2] * along_three)


def closure_adjoint(state_part, assembled, w_in, b_in, w_mid, b_mid, w_out):
    highest = lax.Precision.HIGHEST
    inputs = state_part.astype(jnp.float32)
    pre_first = jnp.einsum('fp,fh->hp', inputs, w_in.astype(jnp.float32), precision=highest) + b_in.astype(jnp.float32)[:, None]
    first = jnp.tanh(pre_first).astype(jnp.bfloat16).astype(jnp.float32)
    pre_second = jnp.einsum('gp,gh->hp', first, w_mid.astype(jnp.float32), precision=highest) + b_mid.astype(jnp.float32)[:, None]
    second = jnp.tanh(pre_second).astype(jnp.bfloat16).astype(jnp.float32)
    impulse = (step_scale * assembled).astype(jnp.bfloat16).astype(jnp.float32)
    back_second = jnp.einsum('hf,ofp->ohp', w_out.astype(jnp.float32), impulse, precision=highest) * (1.0 - second * second)[None]
    back_second = back_second.astype(jnp.bfloat16).astype(jnp.float32)
    back_first = jnp.einsum('gh,ohp->ogp', w_mid.astype(jnp.float32), back_second, precision=highest) * (1.0 - first * first)[None]
    back_first = back_first.astype(jnp.bfloat16).astype(jnp.float32)
    toward = jnp.einsum('fg,ogp->ofp', w_in.astype(jnp.float32), back_first, precision=highest)
    grad_in = jnp.einsum('fp,ogp->fg', inputs, back_first, precision=highest)
    grad_mid = jnp.einsum('gp,ohp->gh', first, back_second, precision=highest)
    grad_out = jnp.einsum('hp,ofp->hf', second, impulse, precision=highest)
    return toward, (grad_in, grad_mid, grad_out)


def reference(state, cotangent, diffusivity, shared_nodes, w_in, b_in, w_mid, b_mid, w_out):
    local = E_DEV * NODES
    valid = shared_nodes >= 0
    safe = jnp.maximum(shared_nodes, 0).astype(jnp.int32)
    ranks = jnp.arange(PARTS_SIZE, dtype=jnp.int32)
    home = (ranks[:, None, None] * local + safe).reshape(-1).astype(jnp.int32)
    shared = jnp.zeros((POINTS,), jnp.float32).at[home].max(valid.reshape(-1).astype(jnp.float32))
    scaled = cotangent / (1.0 + shared)[None, None, :]
    assembled = scaled
    for which, offset in enumerate(peer_offsets()):
        peer = jnp.clip(ranks + offset, 0, PARTS_SIZE - 1).astype(jnp.int32)
        source = (peer[:, None] * local + safe[peer, which ^ 1]).reshape(-1).astype(jnp.int32)
        target = (ranks[:, None] * local + safe[:, which]).reshape(-1).astype(jnp.int32)
        weight = valid[:, which].reshape(-1).astype(jnp.float32)
        assembled = assembled.at[:, :, target].add(scaled[:, :, source] * weight[None, None, :])
    parts_cot = assembled.reshape(OBJECTIVES, FIELDS, PARTS_SIZE, local).transpose(2, 0, 1, 3)
    parts_state = state.reshape(FIELDS, PARTS_SIZE, local).transpose(1, 0, 2)
    parts_diff = diffusivity.reshape(3, PARTS_SIZE, E_DEV).transpose(1, 0, 2)

    def one_part(items):
        state_part, cot_part, diff_part = items
        blocks = cot_part.reshape(OBJECTIVES * FIELDS, E_DEV, 8, 8, 8)
        viscous = diffuse(blocks, diff_part).reshape(cot_part.shape)
        toward, grads = closure_adjoint(state_part, cot_part, w_in, b_in, w_mid, b_mid, w_out)
        return cot_part + step_scale * viscous + toward, grads

    results, grads = lax.map(one_part, (parts_state, parts_cot, parts_diff))
    grad_state = results.transpose(1, 2, 0, 3).reshape(OBJECTIVES, FIELDS, POINTS)
    return grad_state, jnp.sum(grads[0], axis=0), jnp.sum(grads[1], axis=0), jnp.sum(grads[2], axis=0)
```

```python
import jax
import jax.numpy as jnp
import numpy as np
import ml_dtypes
from jax import lax
from jax.experimental import pallas as pl
from jax.experimental.pallas import tpu as pltpu
from jax.sharding import PartitionSpec as P

FIELDS = 14
ROWS = 16
HIDDEN = 128
NODES = 512
ELEMS = 8
LANES = 128
LOCAL = ELEMS * NODES
CHUNKS = LOCAL // LANES
PROWS = 4
SLOTS = 384
FACE_BLOCKS = 12
BLOCKS = 14
PIECE = 5
MESH = pl.DeviceIdType.MESH
OFFSETS = (1, -1, PROWS, -PROWS, PROWS + 1, -PROWS - 1, PROWS - 1, -PROWS + 1)
ZBLOCK = 4

step_scale = 0.5


def stiffness_table():
    order = 7
    points = np.cos(np.pi * np.arange(order + 1) / order)
    ends = np.ones(order + 1)
    ends[0] = 2.0
    ends[-1] = 2.0
    deriv = np.zeros((order + 1, order + 1))
    for first in range(order + 1):
        for second in range(order + 1):
            if first != second:
                deriv[first, second] = (
                    ends[first]
                    / ends[second]
                    * (-1.0) ** (first + second)
                    / (points[first] - points[second])
                )
    row_sums = deriv.sum(axis=1)
    for place in range(order + 1):
        deriv[place, place] = -row_sums[place]
    return deriv.T @ deriv


def split_table(table):
    high = table.astype(ml_dtypes.bfloat16)
    low = (table - high.astype(np.float64)).astype(ml_dtypes.bfloat16)
    return np.stack([high, low])


def direction_tables():
    table = stiffness_table()
    along_one = np.kron(table, np.eye(64)).T
    along_two = np.kron(np.eye(2), np.kron(table, np.eye(8))).T
    along_three = np.kron(np.eye(16), table).T
    return split_table(along_one), split_table(np.concatenate([along_two, along_three], axis=1))


def pick(block, places):
    return jnp.take_along_axis(block, places, axis=1, mode="promise_in_bounds")


def contract(left, right, left_dim, right_dim):
    return lax.dot_general(
        left,
        right,
        (((left_dim,), (right_dim,)), ((), ())),
        preferred_element_type=jnp.float32,
    )


def span(which, size):
    return pl.ds(pl.multiple_of(which * size, size), size)


def body(
    state,
    cot,
    diff,
    lists,
    w_in,
    b_in,
    w_mid,
    b_mid,
    w_out,
    one_hbm,
    two_three,
    out,
    gin,
    gmid,
    gout,
    cot16,
    send_idx,
    send_blocks,
    face_in,
    diag_in,
    slot_high,
    slot_low,
    inv_block,
    inv_lane,
    asm,
    firsts,
    seconds,
    back_firsts,
    grads,
    pieces,
    rs1,
    rs2,
    mine,
    ring_a,
    ring_b,
    final,
    one_vmem,
    table_sem,
    halo_send,
    halo_recv,
    rs1_send,
    rs1_recv,
    rs2_send,
    rs2_recv,
    a_send,
    a_recv,
    b_send,
    b_recv,
    g1_send,
    g1_recv,
    g2_send,
    g2_recv,
    far_one,
    far_two,
):
    graph = lax.axis_index("graph")
    x = lax.axis_index("group")
    z = graph // 8
    q = graph % 8
    zl = z % ZBLOCK
    zh = z // ZBLOCK
    outer = 32 // ZBLOCK

    def place(z_at, q_at, x_at):
        return {"graph": z_at * 8 + q_at, "group": x_at}

    def beside(offset):
        return {"graph": (graph + offset + 256) % 256, "group": x}

    def in_plane(d):
        return place(z, (q + d) % 8, x)

    def along_x(d):
        return place(z, q, (x + d) % 4)

    def in_block(d):
        return place(zh * ZBLOCK + (zl + d) % ZBLOCK, q, x)

    def across(d):
        return place(((zh + d) % outer) * ZBLOCK + zl, q, x)

    def along_z(d):
        return place((z + d + 32) % 32, q, x)

    table_copy = pltpu.make_async_copy(one_hbm, one_vmem, table_sem)
    table_copy.start()

    barrier = pltpu.get_barrier_semaphore()
    near = [beside(o) for o in OFFSETS]
    near += [in_plane(d) for d in range(1, 8)]
    near += [along_x(d) for d in range(1, 4)]
    near += [in_block(d) for d in range(1, ZBLOCK)]
    near += [along_z(4), along_z(-4)]
    for target in near:
        pl.semaphore_signal(barrier, inc=1, device_id=target, device_id_type=MESH)

    cot16[0:FIELDS, :] = cot[0]
    cot16[FIELDS:ROWS, :] = jnp.zeros((ROWS - FIELDS, LOCAL), jnp.float32)
    lane = lax.broadcasted_iota(jnp.int32, (1, LANES), 1)
    leading = lane < 64

    def list_row(which, block):
        return lists[0, which : which + 1, block * LANES : (block + 1) * LANES]

    sent, received = [], []
    for b in range(FACE_BLOCKS):
        row = list_row(b // 3, b % 3)
        sent.append(row)
        received.append(row)
    for k in (4, 6):
        low, high = list_row(k, 0), list_row(k + 1, 0)
        sent.append(jnp.where(leading, low, pltpu.roll(high, 64, 1)))
        received.append(jnp.where(leading, high, pltpu.roll(low, 64, 1)))
    for b in range(BLOCKS):
        send_idx[b] = jnp.broadcast_to(sent[b], (8, LANES))

    def gather_block(b, carry):
        idx = send_idx[b]
        low = jnp.bitwise_and(idx, LANES - 1)
        high = jnp.right_shift(idx, 7)
        top = jnp.zeros((8, LANES), jnp.float32)
        bottom = jnp.zeros((8, LANES), jnp.float32)
        for h in range(CHUNKS):
            match = high == h
            lanes = slice(h * LANES, (h + 1) * LANES)
            top = jnp.where(match, pick(cot16[0:8, lanes], low), top)
            bottom = jnp.where(match, pick(cot16[8:16, lanes], low), bottom)
        send_blocks[b, 0:8] = top
        send_blocks[b, 8:16] = bottom
        return carry

    lax.fori_loop(0, BLOCKS, gather_block, 0)

    pl.semaphore_wait(barrier, len(near))
    halo = []
    for k in range(8):
        if k < 4:
            source = send_blocks.at[3 * k : 3 * k + 3]
            target = face_in.at[3 * (k ^ 1) : 3 * (k ^ 1) + 3]
        else:
            source = send_blocks.at[FACE_BLOCKS + (k - 4) // 2]
            target = diag_in.at[(k ^ 1) - 4]
        copy = pltpu.make_async_remote_copy(
            src_ref=source,
            dst_ref=target,
            send_sem=halo_send.at[k],
            recv_sem=halo_recv.at[k ^ 1],
            device_id=beside(OFFSETS[k]),
            device_id_type=MESH,
        )
        copy.start()
        halo.append(copy)
    for d in (4, -4):
        pl.semaphore_signal(far_one, inc=1, device_id=along_z(d), device_id_type=MESH)

    lane_f = lane.astype(jnp.float32)
    rows32 = lax.broadcasted_iota(jnp.int32, (CHUNKS, LANES), 0)
    rows128 = lax.broadcasted_iota(jnp.int32, (LANES, LANES), 0)
    for b in range(BLOCKS):
        low = jnp.bitwise_and(received[b], LANES - 1)
        high = jnp.right_shift(received[b], 7)
        match = rows32 == high
        lanes = slice(b * LANES, (b + 1) * LANES)
        slot_high[0:32, lanes] = jnp.where(match, float(b + 1), 0.0).astype(jnp.bfloat16)
        slot_high[32:64, lanes] = jnp.where(match, lane_f, 0.0).astype(jnp.bfloat16)
        slot_low[:, lanes] = jnp.where(rows128 == low, 1.0, 0.0).astype(jnp.bfloat16)
    inverse = contract(slot_high[...], slot_low[...], 1, 1).astype(jnp.int32)
    for h in range(CHUNKS):
        inv_block[h] = jnp.broadcast_to(inverse[h : h + 1], (8, LANES))
        inv_lane[h] = jnp.broadcast_to(inverse[32 + h : 33 + h], (8, LANES))

    bias_in = jnp.broadcast_to(b_in[...].reshape(1, HIDDEN), (HIDDEN, HIDDEN)).T[:, 0:1]
    bias_mid = jnp.broadcast_to(b_mid[...].reshape(1, HIDDEN), (HIDDEN, HIDDEN)).T[:, 0:1]

    def forward(e, carry):
        inputs = state[:, span(e, NODES)]
        first = jnp.tanh(contract(w_in[...], inputs, 0, 0) + bias_in).astype(jnp.bfloat16)
        firsts[e] = first
        second = jnp.tanh(contract(w_mid[...], first, 0, 0) + bias_mid).astype(jnp.bfloat16)
        seconds[e] = second
        return carry

    lax.fori_loop(0, ELEMS, forward, 0)

    pl.semaphore_wait(far_one, 2)
    for d in (8, -8):
        pl.semaphore_signal(far_two, inc=1, device_id=along_z(d), device_id_type=MESH)

    for copy in halo:
        copy.wait_recv()

    def assemble(h, carry):
        where_block = inv_block[h]
        where_lane = inv_lane[h]
        top = jnp.zeros((8, LANES), jnp.float32)
        bottom = jnp.zeros((8, LANES), jnp.float32)
        for b in range(BLOCKS):
            match = where_block == b + 1
            if b < FACE_BLOCKS:
                upper, lower = face_in[b, 0:8], face_in[b, 8:16]
            else:
                k = 2 * (b - FACE_BLOCKS)
                upper = jnp.where(leading, diag_in[k + 1, 0:8], diag_in[k, 0:8])
                lower = jnp.where(leading, diag_in[k + 1, 8:16], diag_in[k, 8:16])
            top = jnp.where(match, pick(upper, where_lane), top)
            bottom = jnp.where(match, pick(lower, where_lane), bottom)
        shared = where_block > 0
        own = cot16[0:8, span(h, LANES)]
        asm[0:8, span(h, LANES)] = jnp.where(shared, 0.5 * own + 0.5 * top, own)
        own = cot16[8:16, span(h, LANES)]
        asm[8:16, span(h, LANES)] = jnp.where(shared, 0.5 * own + 0.5 * bottom, own)
        return carry

    lax.fori_loop(0, CHUNKS, assemble, 0)

    grads[...] = jnp.zeros_like(grads)

    def backward(e, carry):
        here = span(e, NODES)
        impulse = (step_scale * asm[0:FIELDS, here]).astype(jnp.bfloat16)
        first, second = firsts[e], seconds[e]
        wide = second.astype(jnp.float32)
        back_second = contract(w_out[...], impulse, 1, 0) * (1.0 - wide * wide)
        back_second = back_second.astype(jnp.bfloat16)
        wide = first.astype(jnp.float32)
        back_first = contract(w_mid[...], back_second, 1, 0) * (1.0 - wide * wide)
        back_first = back_first.astype(jnp.bfloat16)
        back_firsts[e] = back_first
        grads[0:128] += contract(first, back_second, 1, 1)
        grads[128 : 128 + FIELDS] += contract(state[:, here], back_first, 1, 1)
        grads[144 : 144 + FIELDS] += contract(impulse, second, 1, 1)
        return carry

    lax.fori_loop(0, ELEMS, backward, 0)

    for r in range(32):
        pieces[r // 4, r % 4] = grads[PIECE * r : PIECE * (r + 1)]
    sends = []

    def push(source, target, send_sem, recv_sem, device):
        copy = pltpu.make_async_remote_copy(
            src_ref=source,
            dst_ref=target,
            send_sem=send_sem,
            recv_sem=recv_sem,
            device_id=device,
            device_id_type=MESH,
        )
        copy.start()
        sends.append(copy)
        return copy

    arriving = [
        push(pieces.at[(q + d) % 8], rs1.at[d - 1], rs1_send.at[d - 1], rs1_recv.at[d - 1], in_plane(d))
        for d in range(1, 8)
    ]
    total = pieces[q]
    for d in range(1, 8):
        arriving[d - 1].wait_recv()
        total = total + rs1[d - 1]
    mine[...] = total
    arriving = [
        push(mine.at[(x + d) % 4], rs2.at[d - 1], rs2_send.at[d - 1], rs2_recv.at[d - 1], along_x(d))
        for d in range(1, 4)
    ]
    total = mine[x]
    for d in range(1, 4):
        arriving[d - 1].wait_recv()
        total = total + rs2[d - 1]

    ring_a[zl] = total
    arriving = [
        push(ring_a.at[zl], ring_a.at[zl], a_send.at[d - 1], a_recv.at[d - 1], in_block(d))
        for d in range(1, ZBLOCK)
    ]
    for copy in arriving:
        copy.wait_recv()
    total = ring_a[0]
    for d in range(1, ZBLOCK):
        total = total + ring_a[d]
    ring_b[zh] = total
    pl.semaphore_wait(far_two, 2)
    across_z = [
        push(ring_b.at[zh], ring_b.at[zh], b_send.at[d - 1], b_recv.at[d - 1], across(d))
        for d in range(1, outer)
    ]

    table_copy.wait()
    rows = jnp.concatenate([asm[:, e * NODES : (e + 1) * NODES] for e in range(ELEMS)], axis=0)
    high = rows.astype(jnp.bfloat16)
    low = (rows - high.astype(jnp.float32)).astype(jnp.bfloat16)
    along_one = (
        contract(high, one_vmem[0], 1, 0)
        + contract(low, one_vmem[0], 1, 0)
        + contract(high, one_vmem[1], 1, 0)
    )
    for e in range(ELEMS):
        toward = contract(w_in[...], back_firsts[e], 1, 0)
        for part in range(NODES // LANES):
            lanes = slice(part * LANES, (part + 1) * LANES)
            high_here = high[e * ROWS : (e + 1) * ROWS, lanes]
            low_here = low[e * ROWS : (e + 1) * ROWS, lanes]
            others = (
                contract(high_here, two_three[0], 1, 0)
                + contract(low_here, two_three[0], 1, 0)
                + contract(high_here, two_three[1], 1, 0)
            )
            viscous = -(
                diff[0, e] * along_one[e * ROWS : (e + 1) * ROWS, lanes]
                + diff[1, e] * others[:, 0:LANES]
                + diff[2, e] * others[:, LANES:]
            )
            here = slice(e * NODES + part * LANES, e * NODES + (part + 1) * LANES)
            value = asm[:, here] + step_scale * viscous
            out[0, :, here] = value[0:FIELDS] + toward[:, lanes]

    for copy in across_z:
        copy.wait_recv()
    total = ring_b[0]
    for d in range(1, outer):
        total = total + ring_b[d]

    final[q, x] = total
    arriving = [
        push(final.at[q, x], final.at[q, x], g1_send.at[d - 1], g1_recv.at[d - 1], along_x(d))
        for d in range(1, 4)
    ]
    for copy in arriving:
        copy.wait_recv()
    arriving = [
        push(final.at[q], final.at[q], g2_send.at[d - 1], g2_recv.at[d - 1], in_plane(d))
        for d in range(1, 8)
    ]
    for copy in arriving:
        copy.wait_recv()
    for r in range(32):
        grads[PIECE * r : PIECE * (r + 1)] = final[r // 4, r % 4]
    gmid[...] = grads[0:128]
    gin[...] = grads[128 : 128 + FIELDS]
    gout[...] = grads[144:160].T[:, 0:FIELDS]

    for copy in halo + sends:
        copy.wait_send()


def per_device(state, cotangent, diffusivity, shared_nodes, w_in, b_in, w_mid, b_mid, w_out):
    f32, bf16 = jnp.float32, jnp.bfloat16
    one, two_three = direction_tables()
    vmem = pl.BlockSpec(memory_space=pltpu.VMEM)
    dma = pltpu.SemaphoreType.DMA
    outer = 32 // ZBLOCK
    return pl.pallas_call(
        body,
        out_shape=(
            jax.ShapeDtypeStruct((1, FIELDS, LOCAL), f32),
            jax.ShapeDtypeStruct((FIELDS, HIDDEN), f32),
            jax.ShapeDtypeStruct((HIDDEN, HIDDEN), f32),
            jax.ShapeDtypeStruct((HIDDEN, FIELDS), f32),
        ),
        in_specs=[vmem, vmem, pl.BlockSpec(memory_space=pltpu.SMEM)]
        + [vmem] * 6
        + [pl.BlockSpec(memory_space=pl.ANY), vmem],
        out_specs=(vmem, vmem, vmem, vmem),
        scratch_shapes=[
            pltpu.VMEM((ROWS, LOCAL), f32),
            pltpu.VMEM((BLOCKS, 8, LANES), jnp.int32),
            pltpu.VMEM((BLOCKS, ROWS, LANES), f32),
            pltpu.VMEM((FACE_BLOCKS, ROWS, LANES), f32),
            pltpu.VMEM((4, ROWS, LANES), f32),
            pltpu.VMEM((64, BLOCKS * LANES), bf16),
            pltpu.VMEM((LANES, BLOCKS * LANES), bf16),
            pltpu.VMEM((CHUNKS, 8, LANES), jnp.int32),
            pltpu.VMEM((CHUNKS, 8, LANES), jnp.int32),
            pltpu.VMEM((ROWS, LOCAL), f32),
            pltpu.VMEM((ELEMS, HIDDEN, NODES), bf16),
            pltpu.VMEM((ELEMS, HIDDEN, NODES), bf16),
            pltpu.VMEM((ELEMS, HIDDEN, NODES), bf16),
            pltpu.VMEM((160, HIDDEN), f32),
            pltpu.VMEM((8, 4, PIECE, LANES), f32),
            pltpu.VMEM((7, 4, PIECE, LANES), f32),
            pltpu.VMEM((3, PIECE, LANES), f32),
            pltpu.VMEM((4, PIECE, LANES), f32),
            pltpu.VMEM((ZBLOCK, PIECE, LANES), f32),
            pltpu.VMEM((outer, PIECE, LANES), f32),
            pltpu.VMEM((8, 4, PIECE, LANES), f32),
            pltpu.VMEM((2, NODES, NODES), bf16),
            dma,
            dma((8,)),
            dma((8,)),
            dma((7,)),
            dma((7,)),
            dma((3,)),
            dma((3,)),
            dma((ZBLOCK - 1,)),
            dma((ZBLOCK - 1,)),
            dma((outer - 1,)),
            dma((outer - 1,)),
            dma((3,)),
            dma((3,)),
            dma((7,)),
            dma((7,)),
            pltpu.SemaphoreType.REGULAR,
            pltpu.SemaphoreType.REGULAR,
        ],
        compiler_params=pltpu.CompilerParams(
            collective_id=0, has_side_effects=True, vmem_limit_bytes=32 * 1024 * 1024
        ),
    )(
        state,
        cotangent,
        diffusivity,
        shared_nodes,
        w_in,
        b_in,
        w_mid,
        b_mid,
        w_out,
        jnp.asarray(one),
        jnp.asarray(two_three),
    )


def solution(mesh):
    in_specs = (
        P(None, "graph"),
        P("group", None, "graph"),
        P(None, "graph"),
        P("graph", None, None),
        P(),
        P(),
        P(),
        P(),
        P(),
    )
    out_specs = (P("group", None, "graph"), P(), P(), P())
    return jax.shard_map(
        per_device, mesh=mesh, in_specs=in_specs, out_specs=out_specs, check_vma=False
    )
```

```python
import jax
import jax.numpy as jnp
import numpy as np
import ml_dtypes
from jax import lax
from jax.experimental import pallas as pl
from jax.experimental.pallas import tpu as pltpu
from jax.sharding import PartitionSpec as P

FIELDS = 14
ROWS = 16
HIDDEN = 128
NODES = 512
ELEMS = 8
LANES = 128
LOCAL = ELEMS * NODES
CHUNKS = LOCAL // LANES
PROWS = 4
SLOTS = 384
FACE_BLOCKS = 12
BLOCKS = 14
PIECE = 5
MESH = pl.DeviceIdType.MESH
OFFSETS = (1, -1, PROWS, -PROWS, PROWS + 1, -PROWS - 1, PROWS - 1, -PROWS + 1)
ZBLOCK = 1
OUTER = 32 // ZBLOCK
NEAR_Z = (1, 2, 3, 4, -1, -2, -3, -4)

step_scale = 0.5


def stiffness_table():
    order = 7
    points = np.cos(np.pi * np.arange(order + 1) / order)
    ends = np.ones(order + 1)
    ends[0] = 2.0
    ends[-1] = 2.0
    deriv = np.zeros((order + 1, order + 1))
    for first in range(order + 1):
        for second in range(order + 1):
            if first != second:
                deriv[first, second] = (
                    ends[first]
                    / ends[second]
                    * (-1.0) ** (first + second)
                    / (points[first] - points[second])
                )
    row_sums = deriv.sum(axis=1)
    for place in range(order + 1):
        deriv[place, place] = -row_sums[place]
    return deriv.T @ deriv


def split_table(table):
    high = table.astype(ml_dtypes.bfloat16)
    low = (table - high.astype(np.float64)).astype(ml_dtypes.bfloat16)
    return np.stack([high, low])


def direction_tables():
    table = stiffness_table()
    along_one = np.kron(table, np.eye(64)).T
    along_two = np.kron(np.eye(2), np.kron(table, np.eye(8))).T
    along_three = np.kron(np.eye(16), table).T
    return split_table(along_one), split_table(np.concatenate([along_two, along_three], axis=1))


def pick(block, places):
    return jnp.take_along_axis(block, places, axis=1, mode="promise_in_bounds")


def contract(left, right, left_dim, right_dim):
    return lax.dot_general(
        left,
        right,
        (((left_dim,), (right_dim,)), ((), ())),
        preferred_element_type=jnp.float32,
    )


def span(which, size):
    return pl.ds(pl.multiple_of(which * size, size), size)


def body(
    state_hbm,
    cot_hbm,
    diff_hbm,
    lists_hbm,
    w_in_hbm,
    b_in_hbm,
    w_mid_hbm,
    b_mid_hbm,
    w_out_hbm,
    one_hbm,
    two_three_hbm,
    out,
    final,
    state,
    cot,
    diff,
    lists,
    w_in,
    b_in,
    w_mid,
    b_mid,
    w_out,
    one,
    two_three,
    cot16,
    send_idx,
    send_blocks,
    face_in,
    diag_in,
    slot_high,
    slot_low,
    inv_block,
    inv_lane,
    asm,
    firsts,
    seconds,
    back_firsts,
    grads,
    pieces,
    plane_in,
    ring_a,
    ring_b,
    fetched,
    halo_send,
    halo_recv,
    rs_send,
    rs_recv,
    a_send,
    a_recv,
    b_send,
    b_recv,
    g_send,
    g_recv,
    far_one,
    far_two,
):
    graph = lax.axis_index("graph")
    x = lax.axis_index("group")
    z = graph // 8
    q = graph % 8
    rank = x * 8 + q
    zl = z % ZBLOCK
    zh = z // ZBLOCK

    def place(z_at, q_at, x_at):
        return {"graph": z_at * 8 + q_at, "group": x_at}

    def beside(offset):
        return {"graph": (graph + offset + 256) % 256, "group": x}

    def in_plane(d):
        other = (rank + d) % 32
        return place(z, other % 8, other // 8)

    def in_block(d):
        return place(zh * ZBLOCK + (zl + d) % ZBLOCK, q, x)

    def across(d):
        return place(((zh + d) % OUTER) * ZBLOCK + zl, q, x)

    def along_z(d):
        return place((z + d + 32) % 32, q, x)

    def signal(semaphore, target):
        pl.semaphore_signal(semaphore, inc=1, device_id=target, device_id_type=MESH)

    fetches = [
        pltpu.make_async_copy(source, target, fetched.at[i])
        for i, (source, target) in enumerate(
            (
                (cot_hbm, cot),
                (lists_hbm, lists),
                (state_hbm, state),
                (w_in_hbm, w_in),
                (b_in_hbm, b_in),
                (w_mid_hbm, w_mid),
                (b_mid_hbm, b_mid),
                (w_out_hbm, w_out),
                (diff_hbm, diff),
                (one_hbm, one),
                (two_three_hbm, two_three),
            )
        )
    ]
    for fetch in fetches:
        fetch.start()

    barrier = pltpu.get_barrier_semaphore()
    near = [beside(o) for o in OFFSETS]
    near += [along_z(d) for d in NEAR_Z]
    near += [in_plane(d) for d in range(1, 32)]
    for target in near:
        signal(barrier, target)

    fetches[0].wait()
    for h in range(CHUNKS):
        cot16[0:FIELDS, h * LANES : (h + 1) * LANES] = cot[pl.ds(h, FIELDS, stride=CHUNKS), :]
    cot16[FIELDS:ROWS, :] = jnp.zeros((ROWS - FIELDS, LOCAL), jnp.float32)
    fetches[1].wait()
    lane = lax.broadcasted_iota(jnp.int32, (1, LANES), 1)
    leading = lane < 64

    def list_row(which, block):
        return lists[0, which : which + 1, block * LANES : (block + 1) * LANES]

    sent, received = [], []
    for b in range(FACE_BLOCKS):
        row = list_row(b // 3, b % 3)
        sent.append(row)
        received.append(row)
    for k in (4, 6):
        low, high = list_row(k, 0), list_row(k + 1, 0)
        sent.append(jnp.where(leading, low, pltpu.roll(high, 64, 1)))
        received.append(jnp.where(leading, high, pltpu.roll(low, 64, 1)))
    for b in range(BLOCKS):
        send_idx[b] = jnp.broadcast_to(sent[b], (8, LANES))

    def gather_block(b, carry):
        idx = send_idx[b]
        low = jnp.bitwise_and(idx, LANES - 1)
        high = jnp.right_shift(idx, 7)
        top = jnp.zeros((8, LANES), jnp.float32)
        bottom = jnp.zeros((8, LANES), jnp.float32)
        for h in range(CHUNKS):
            match = high == h
            lanes = slice(h * LANES, (h + 1) * LANES)
            top = jnp.where(match, pick(cot16[0:8, lanes], low), top)
            bottom = jnp.where(match, pick(cot16[8:16, lanes], low), bottom)
        send_blocks[b, 0:8] = top
        send_blocks[b, 8:16] = bottom
        return carry

    lax.fori_loop(0, BLOCKS, gather_block, 0, unroll=2)

    sends = []

    def push(source, target, send_sem, recv_sem, device):
        copy = pltpu.make_async_remote_copy(
            src_ref=source,
            dst_ref=target,
            send_sem=send_sem,
            recv_sem=recv_sem,
            device_id=device,
            device_id_type=MESH,
        )
        copy.start()
        sends.append(copy)
        return copy

    pl.semaphore_wait(barrier, len(near))
    halo = []
    for k in (2, 3, 0, 1, 4, 5, 6, 7):
        if k < 4:
            source = send_blocks.at[3 * k : 3 * k + 3, 0:FIELDS]
            target = face_in.at[3 * (k ^ 1) : 3 * (k ^ 1) + 3, 0:FIELDS]
        else:
            source = send_blocks.at[FACE_BLOCKS + (k - 4) // 2, 0:FIELDS]
            target = diag_in.at[(k ^ 1) - 4, 0:FIELDS]
        halo.append(push(source, target, halo_send.at[k], halo_recv.at[k ^ 1], beside(OFFSETS[k])))
    for d in (4, -4):
        signal(far_one, along_z(d))

    lane_f = lane.astype(jnp.float32)
    rows32 = lax.broadcasted_iota(jnp.int32, (CHUNKS, LANES), 0)
    rows128 = lax.broadcasted_iota(jnp.int32, (LANES, LANES), 0)
    for b in range(BLOCKS):
        low = jnp.bitwise_and(received[b], LANES - 1)
        high = jnp.right_shift(received[b], 7)
        match = rows32 == high
        lanes = slice(b * LANES, (b + 1) * LANES)
        slot_high[0:32, lanes] = jnp.where(match, float(b + 1), 0.0).astype(jnp.bfloat16)
        slot_high[32:64, lanes] = jnp.where(match, lane_f, 0.0).astype(jnp.bfloat16)
        slot_low[:, lanes] = jnp.where(rows128 == low, 1.0, 0.0).astype(jnp.bfloat16)
    inverse = contract(slot_high[...], slot_low[...], 1, 1).astype(jnp.int32)
    for h in range(CHUNKS):
        inv_block[h] = jnp.broadcast_to(inverse[h : h + 1], (8, LANES))
        inv_lane[h] = jnp.broadcast_to(inverse[32 + h : 33 + h], (8, LANES))

    for fetch in fetches[2:8]:
        fetch.wait()
    bias_in = jnp.broadcast_to(b_in[...].reshape(1, HIDDEN), (HIDDEN, HIDDEN)).T[:, 0:1]
    bias_mid = jnp.broadcast_to(b_mid[...].reshape(1, HIDDEN), (HIDDEN, HIDDEN)).T[:, 0:1]

    def forward(e, carry):
        inputs = state[:, span(e, NODES)]
        first = jnp.tanh(contract(w_in[...], inputs, 0, 0) + bias_in).astype(jnp.bfloat16)
        firsts[e] = first
        second = jnp.tanh(contract(w_mid[...], first, 0, 0) + bias_mid).astype(jnp.bfloat16)
        seconds[e] = second
        return carry

    lax.fori_loop(0, ELEMS, forward, 0)

    pl.semaphore_wait(far_one, 2)
    for d in (8, -8):
        signal(far_two, along_z(d))

    for copy in halo:
        copy.wait_recv()

    def assemble(h, carry):
        where_block = inv_block[h]
        where_lane = inv_lane[h]
        top = jnp.zeros((8, LANES), jnp.float32)
        bottom = jnp.zeros((8, LANES), jnp.float32)
        for b in range(BLOCKS):
            match = where_block == b + 1
            if b < FACE_BLOCKS:
                upper, lower = face_in[b, 0:8], face_in[b, 8:16]
            else:
                k = 2 * (b - FACE_BLOCKS)
                upper = jnp.where(leading, diag_in[k + 1, 0:8], diag_in[k, 0:8])
                lower = jnp.where(leading, diag_in[k + 1, 8:16], diag_in[k, 8:16])
            top = jnp.where(match, pick(upper, where_lane), top)
            bottom = jnp.where(match, pick(lower, where_lane), bottom)
        shared = where_block > 0
        own = cot16[0:8, span(h, LANES)]
        asm[0:8, span(h, LANES)] = jnp.where(shared, 0.5 * own + 0.5 * top, own)
        own = cot16[8:16, span(h, LANES)]
        asm[8:16, span(h, LANES)] = jnp.where(shared, 0.5 * own + 0.5 * bottom, own)
        return carry

    lax.fori_loop(0, CHUNKS, assemble, 0, unroll=2)

    grads[...] = jnp.zeros_like(grads)

    def backward(e, carry):
        here = span(e, NODES)
        impulse = (step_scale * asm[0:FIELDS, here]).astype(jnp.bfloat16)
        first, second = firsts[e], seconds[e]
        wide = second.astype(jnp.float32)
        back_second = contract(w_out[...], impulse, 0, 0) * (1.0 - wide * wide)
        back_second = back_second.astype(jnp.bfloat16)
        wide = first.astype(jnp.float32)
        back_first = contract(w_mid[...], back_second, 1, 0) * (1.0 - wide * wide)
        back_first = back_first.astype(jnp.bfloat16)
        back_firsts[e] = back_first
        grads[0:128] += contract(first, back_second, 1, 1)
        grads[128 : 128 + FIELDS] += contract(state[:, here], back_first, 1, 1)
        grads[144 : 144 + FIELDS] += contract(impulse, second, 1, 1)
        return carry

    lax.fori_loop(0, ELEMS, backward, 0)

    for r in range(32):
        pieces[r] = grads[PIECE * r : PIECE * (r + 1)]
    arriving = [
        push(
            pieces.at[(rank + d) % 32],
            plane_in.at[d - 1],
            rs_send.at[d - 1],
            rs_recv.at[d - 1],
            in_plane(d),
        )
        for d in range(1, 32)
    ]
    total = pieces[rank]
    for d in range(1, 32):
        arriving[d - 1].wait_recv()
        total = total + plane_in[d - 1]

    if ZBLOCK > 1:
        ring_a[zl] = total
        arriving = [
            push(ring_a.at[zl], ring_a.at[zl], a_send.at[d - 1], a_recv.at[d - 1], in_block(d))
            for d in range(1, ZBLOCK)
        ]
        for copy in arriving:
            copy.wait_recv()
        total = ring_a[0]
        for d in range(1, ZBLOCK):
            total = total + ring_a[d]
    ring_b[zh] = total
    pl.semaphore_wait(far_two, 2)
    across_z = [
        push(ring_b.at[zh], ring_b.at[zh], b_send.at[d - 1], b_recv.at[d - 1], across(d))
        for d in sorted(range(1, OUTER), key=lambda d: (-min(d, OUTER - d), d))
    ]

    for fetch in fetches[8:]:
        fetch.wait()
    rows = jnp.concatenate([asm[:, e * NODES : (e + 1) * NODES] for e in range(ELEMS)], axis=0)
    high = rows.astype(jnp.bfloat16)
    low = (rows - high.astype(jnp.float32)).astype(jnp.bfloat16)
    along_one = (
        contract(high, one[0], 1, 0) + contract(low, one[0], 1, 0) + contract(high, one[1], 1, 0)
    )
    for e in range(ELEMS):
        toward = contract(w_in[...], back_firsts[e], 1, 0)
        for part in range(NODES // LANES):
            lanes = slice(part * LANES, (part + 1) * LANES)
            high_here = high[e * ROWS : (e + 1) * ROWS, lanes]
            low_here = low[e * ROWS : (e + 1) * ROWS, lanes]
            others = (
                contract(high_here, two_three[0], 1, 0)
                + contract(low_here, two_three[0], 1, 0)
                + contract(high_here, two_three[1], 1, 0)
            )
            viscous = -(
                diff[0, e] * along_one[e * ROWS : (e + 1) * ROWS, lanes]
                + diff[1, e] * others[:, 0:LANES]
                + diff[2, e] * others[:, LANES:]
            )
            chunk = e * (NODES // LANES) + part
            value = asm[:, chunk * LANES : (chunk + 1) * LANES] + step_scale * viscous
            out[pl.ds(chunk, FIELDS, stride=CHUNKS), :] = value[0:FIELDS] + toward[:, lanes]

    for copy in across_z:
        copy.wait_recv()
    total = ring_b[0]
    for d in range(1, OUTER):
        total = total + ring_b[d]

    final[rank] = total
    arriving = [
        push(final.at[rank], final.at[rank], g_send.at[d - 1], g_recv.at[d - 1], in_plane(d))
        for d in range(1, 32)
    ]
    for copy in arriving:
        copy.wait_recv()
    for copy in sends:
        copy.wait_send()


def finish(state_in, final, state_out, gin, gmid, gout, rows, sem):
    copy = pltpu.make_async_copy(state_in, state_out, sem)
    copy.start()
    for r in range(32):
        rows[PIECE * r : PIECE * (r + 1)] = final[r]
    gmid[...] = rows[0:128]
    gin[...] = rows[128 : 128 + FIELDS]
    gout[...] = rows[144 : 144 + FIELDS]
    copy.wait()


def per_device(state, cotangent, diffusivity, shared_nodes, w_in, b_in, w_mid, b_mid, w_out):
    f32, bf16 = jnp.float32, jnp.bfloat16
    one, two_three = direction_tables()
    vmem = pl.BlockSpec(memory_space=pltpu.VMEM)
    hbm = pl.BlockSpec(memory_space=pltpu.HBM)
    dma = pltpu.SemaphoreType.DMA
    result, final = pl.pallas_call(
        body,
        out_shape=(
            pltpu.VMEM((FIELDS * CHUNKS, LANES), f32),
            pltpu.VMEM((32, PIECE, LANES), f32),
        ),
        in_specs=[hbm] * 11,
        out_specs=(vmem, vmem),
        scratch_shapes=[
            pltpu.VMEM((FIELDS, LOCAL), bf16),
            pltpu.VMEM((FIELDS * CHUNKS, LANES), f32),
            pltpu.SMEM((3, ELEMS), f32),
            pltpu.VMEM((1, 8, SLOTS), jnp.int32),
            pltpu.VMEM((FIELDS, HIDDEN), bf16),
            pltpu.VMEM((HIDDEN,), f32),
            pltpu.VMEM((HIDDEN, HIDDEN), bf16),
            pltpu.VMEM((HIDDEN,), f32),
            pltpu.VMEM((FIELDS, HIDDEN), bf16),
            pltpu.VMEM((2, NODES, NODES), bf16),
            pltpu.VMEM((2, LANES, 2 * LANES), bf16),
            pltpu.VMEM((ROWS, LOCAL), f32),
            pltpu.VMEM((BLOCKS, 8, LANES), jnp.int32),
            pltpu.VMEM((BLOCKS, ROWS, LANES), f32),
            pltpu.VMEM((FACE_BLOCKS, ROWS, LANES), f32),
            pltpu.VMEM((4, ROWS, LANES), f32),
            pltpu.VMEM((64, BLOCKS * LANES), bf16),
            pltpu.VMEM((LANES, BLOCKS * LANES), bf16),
            pltpu.VMEM((CHUNKS, 8, LANES), jnp.int32),
            pltpu.VMEM((CHUNKS, 8, LANES), jnp.int32),
            pltpu.VMEM((ROWS, LOCAL), f32),
            pltpu.VMEM((ELEMS, HIDDEN, NODES), bf16),
            pltpu.VMEM((ELEMS, HIDDEN, NODES), bf16),
            pltpu.VMEM((ELEMS, HIDDEN, NODES), bf16),
            pltpu.VMEM((160, HIDDEN), f32),
            pltpu.VMEM((32, PIECE, LANES), f32),
            pltpu.VMEM((31, PIECE, LANES), f32),
            pltpu.VMEM((ZBLOCK, PIECE, LANES), f32),
            pltpu.VMEM((OUTER, PIECE, LANES), f32),
            dma((11,)),
            dma((8,)),
            dma((8,)),
            dma((31,)),
            dma((31,)),
            dma((max(ZBLOCK - 1, 1),)),
            dma((max(ZBLOCK - 1, 1),)),
            dma((OUTER - 1,)),
            dma((OUTER - 1,)),
            dma((31,)),
            dma((31,)),
            pltpu.SemaphoreType.REGULAR,
            pltpu.SemaphoreType.REGULAR,
        ],
        compiler_params=pltpu.CompilerParams(
            collective_id=0, has_side_effects=True, vmem_limit_bytes=66_500_000
        ),
    )(
        state,
        cotangent.reshape(FIELDS * CHUNKS, LANES),
        diffusivity,
        shared_nodes,
        w_in,
        b_in,
        w_mid,
        b_mid,
        w_out.T,
        jnp.asarray(one),
        jnp.asarray(two_three),
    )
    grad_state, grad_in, grad_mid, grad_out = pl.pallas_call(
        finish,
        out_shape=(
            jax.ShapeDtypeStruct((FIELDS * CHUNKS, LANES), f32),
            jax.ShapeDtypeStruct((FIELDS, HIDDEN), f32),
            jax.ShapeDtypeStruct((HIDDEN, HIDDEN), f32),
            jax.ShapeDtypeStruct((FIELDS, HIDDEN), f32),
        ),
        in_specs=[vmem, vmem],
        out_specs=(hbm, vmem, vmem, vmem),
        scratch_shapes=[pltpu.VMEM((160, HIDDEN), f32), dma],
        compiler_params=pltpu.CompilerParams(vmem_limit_bytes=8 * 1024 * 1024),
    )(result, final)
    return grad_state.reshape(1, FIELDS, LOCAL), grad_in, grad_mid, grad_out.T


def solution(mesh):
    in_specs = (
        P(None, "graph"),
        P("group", None, "graph"),
        P(None, "graph"),
        P("graph", None, None),
        P(),
        P(),
        P(),
        P(),
        P(),
    )
    out_specs = (P("group", None, "graph"), P(), P(), P())
    return jax.shard_map(
        per_device, mesh=mesh, in_specs=in_specs, out_specs=out_specs, check_vma=False
    )
```

```python
import jax
import jax.numpy as jnp
import numpy as np
import ml_dtypes
from jax import lax
from jax.experimental import pallas as pl
from jax.experimental.pallas import tpu as pltpu
from jax.sharding import PartitionSpec as P

FIELDS = 14
ROWS = 16
HIDDEN = 128
NODES = 512
ELEMS = 8
LANES = 128
LOCAL = ELEMS * NODES
CHUNKS = LOCAL // LANES
PROWS = 4
SLOTS = 384
FACE_BLOCKS = 12
BLOCKS = 14
PIECE = 5
MESH = pl.DeviceIdType.MESH
OFFSETS = (1, -1, PROWS, -PROWS, PROWS + 1, -PROWS - 1, PROWS - 1, -PROWS + 1)
PLANE = sorted(
    ((dx, dy, dc) for dx in range(4) for dy in range(4) for dc in range(2) if dx or dy or dc),
    key=lambda step: -min(step[0], 4 - step[0]) - min(step[1], 4 - step[1]),
)
DEPTH = 32
NEAR_Z = (3, -3, 2, -2, 1, -1)

step_scale = 0.5


def stiffness_table():
    order = 7
    points = np.cos(np.pi * np.arange(order + 1) / order)
    ends = np.ones(order + 1)
    ends[0] = 2.0
    ends[-1] = 2.0
    deriv = np.zeros((order + 1, order + 1))
    for first in range(order + 1):
        for second in range(order + 1):
            if first != second:
                deriv[first, second] = (
                    ends[first]
                    / ends[second]
                    * (-1.0) ** (first + second)
                    / (points[first] - points[second])
                )
    row_sums = deriv.sum(axis=1)
    for place in range(order + 1):
        deriv[place, place] = -row_sums[place]
    return deriv.T @ deriv


def split_table(table):
    high = table.astype(ml_dtypes.bfloat16)
    low = (table - high.astype(np.float64)).astype(ml_dtypes.bfloat16)
    return np.stack([high, low])


def direction_tables():
    table = stiffness_table()
    along_one = np.kron(table, np.eye(64)).T
    along_two = np.kron(np.eye(2), np.kron(table, np.eye(8))).T
    along_three = np.kron(np.eye(16), table).T
    return split_table(along_one), split_table(np.concatenate([along_two, along_three], axis=1))


def pick(block, places):
    return jnp.take_along_axis(block, places, axis=1, mode="promise_in_bounds")


def contract(left, right, left_dim, right_dim):
    return lax.dot_general(
        left,
        right,
        (((left_dim,), (right_dim,)), ((), ())),
        preferred_element_type=jnp.float32,
    )


def span(which, size):
    return pl.ds(pl.multiple_of(which * size, size), size)


def body(
    state_hbm,
    cot_hbm,
    diff_hbm,
    lists_hbm,
    w_in_hbm,
    b_in_hbm,
    w_mid_hbm,
    b_mid_hbm,
    w_out_hbm,
    one_hbm,
    two_three_hbm,
    out,
    final,
    state,
    cot,
    diff,
    lists,
    w_in,
    b_in,
    w_mid,
    b_mid,
    w_out,
    one,
    two_three,
    cot16,
    send_idx,
    send_blocks,
    face_in,
    diag_in,
    slot_high,
    slot_low,
    inv_block,
    inv_lane,
    asm,
    firsts,
    seconds,
    first_slopes,
    second_slopes,
    back_firsts,
    grads,
    pieces,
    plane_in,
    along,
    fetched,
    halo_send,
    halo_recv,
    rs_send,
    rs_recv,
    z_send,
    z_recv,
    g_send,
    g_recv,
    plane_here,
    far_one,
    far_two,
    far_three,
):
    graph = lax.axis_index("graph")
    x = lax.axis_index("group")
    z = lax.div(graph, 8)
    q = lax.rem(graph, 8)
    y = lax.div(q, 2)
    core = lax.rem(q, 2)
    rank = x * 8 + q

    def place(z_at, q_at, x_at):
        return {"graph": z_at * 8 + q_at, "group": x_at}

    def beside(offset):
        return {"graph": lax.rem(graph + (offset + 256), 256), "group": x}

    def step_place(step):
        dx, dy, dc = step
        q_at = lax.rem(y + dy, 4) * 2 + lax.rem(core + dc, 2)
        return q_at, lax.rem(x + dx, 4)

    def step_rank(step):
        q_at, x_at = step_place(step)
        return x_at * 8 + q_at

    def in_plane(step):
        return place(z, *step_place(step))

    def along_z(d):
        return place(lax.rem(z + (d + 32), 32), q, x)

    def signal(semaphore, target):
        pl.semaphore_signal(semaphore, inc=1, device_id=target, device_id_type=MESH)

    fetches = [
        pltpu.make_async_copy(source, target, fetched.at[i])
        for i, (source, target) in enumerate(
            (
                (cot_hbm, cot),
                (lists_hbm, lists),
                (state_hbm, state),
                (w_in_hbm, w_in),
                (b_in_hbm, b_in),
                (w_mid_hbm, w_mid),
                (b_mid_hbm, b_mid),
                (w_out_hbm, w_out),
                (diff_hbm, diff),
                (one_hbm, one),
                (two_three_hbm, two_three),
            )
        )
    ]
    for fetch in fetches:
        fetch.start()

    barrier = pltpu.get_barrier_semaphore()
    along_x = [step for step in PLANE if step[1] == step[2] == 0]
    near = [along_z(d) for d in NEAR_Z]
    near += [beside(o) for o in OFFSETS]
    near += [in_plane(step) for step in PLANE if step[0] == 0]
    near += [in_plane(step) for step in along_x]
    for target in near:
        signal(barrier, target)

    fetches[0].wait()
    for h in range(CHUNKS):
        cot16[0:FIELDS, h * LANES : (h + 1) * LANES] = cot[pl.ds(h, FIELDS, stride=CHUNKS), :]
    cot16[FIELDS:ROWS, :] = jnp.zeros((ROWS - FIELDS, LOCAL), jnp.float32)
    fetches[1].wait()
    lane = lax.broadcasted_iota(jnp.int32, (1, LANES), 1)
    leading = lane < 64

    def list_row(which, block):
        return lists[0, which : which + 1, block * LANES : (block + 1) * LANES]

    sent, received = [], []
    for b in range(FACE_BLOCKS):
        row = list_row(b // 3, b % 3)
        sent.append(row)
        received.append(row)
    for k in (4, 6):
        low, high = list_row(k, 0), list_row(k + 1, 0)
        sent.append(jnp.where(leading, low, pltpu.roll(high, 64, 1)))
        received.append(jnp.where(leading, high, pltpu.roll(low, 64, 1)))
    for b in range(BLOCKS):
        send_idx[b] = jnp.broadcast_to(sent[b], (8, LANES))

    def gather_block(b, carry):
        idx = send_idx[b]
        low = jnp.bitwise_and(idx, LANES - 1)
        high = jnp.right_shift(idx, 7)
        top = jnp.zeros((8, LANES), jnp.float32)
        bottom = jnp.zeros((8, LANES), jnp.float32)
        for h in range(CHUNKS):
            match = high == h
            lanes = slice(h * LANES, (h + 1) * LANES)
            top = jnp.where(match, pick(cot16[0:8, lanes], low), top)
            bottom = jnp.where(match, pick(cot16[8:16, lanes], low), bottom)
        send_blocks[b, 0:8] = top
        send_blocks[b, 8:16] = bottom
        return carry

    lax.fori_loop(0, BLOCKS, gather_block, 0, unroll=2)

    sends = []

    def push(source, target, send_sem, recv_sem, device):
        copy = pltpu.make_async_remote_copy(
            src_ref=source,
            dst_ref=target,
            send_sem=send_sem,
            recv_sem=recv_sem,
            device_id=device,
            device_id_type=MESH,
        )
        copy.start()
        sends.append(copy)
        return copy

    pl.semaphore_wait(barrier, len(near))
    halo = []
    for k in (2, 3, 4, 5, 6, 7, 0, 1):
        if k < 4:
            source = send_blocks.at[3 * k : 3 * k + 3, 0:FIELDS]
            target = face_in.at[3 * (k ^ 1) : 3 * (k ^ 1) + 3, 0:FIELDS]
        else:
            source = send_blocks.at[FACE_BLOCKS + (k - 4) // 2, 0:FIELDS]
            target = diag_in.at[(k ^ 1) - 4, 0:FIELDS]
        halo.append(push(source, target, halo_send.at[k], halo_recv.at[k ^ 1], beside(OFFSETS[k])))
    for step in along_x:
        signal(plane_here, in_plane(step))
    for d in (3, -3):
        signal(far_one, along_z(d))

    lane_f = lane.astype(jnp.float32)
    rows32 = lax.broadcasted_iota(jnp.int32, (CHUNKS, LANES), 0)
    rows128 = lax.broadcasted_iota(jnp.int32, (LANES, LANES), 0)
    for b in range(BLOCKS):
        low = jnp.bitwise_and(received[b], LANES - 1)
        high = jnp.right_shift(received[b], 7)
        match = rows32 == high
        lanes = slice(b * LANES, (b + 1) * LANES)
        slot_high[0:32, lanes] = jnp.where(match, float(b + 1), 0.0).astype(jnp.bfloat16)
        slot_high[32:64, lanes] = jnp.where(match, lane_f, 0.0).astype(jnp.bfloat16)
        slot_low[:, lanes] = jnp.where(rows128 == low, 1.0, 0.0).astype(jnp.bfloat16)
    inverse = contract(slot_high[...], slot_low[...], 1, 1).astype(jnp.int32)
    for h in range(CHUNKS):
        inv_block[h] = jnp.broadcast_to(inverse[h : h + 1], (8, LANES))
        inv_lane[h] = jnp.broadcast_to(inverse[32 + h : 33 + h], (8, LANES))

    for fetch in fetches[2:8]:
        fetch.wait()
    bias_in = jnp.broadcast_to(b_in[...].reshape(1, HIDDEN), (HIDDEN, HIDDEN)).T[:, 0:1]
    bias_mid = jnp.broadcast_to(b_mid[...].reshape(1, HIDDEN), (HIDDEN, HIDDEN)).T[:, 0:1]

    def forward(e, carry):
        inputs = state[:, span(e, NODES)]
        first = jnp.tanh(contract(w_in[...], inputs, 0, 0) + bias_in).astype(jnp.bfloat16)
        firsts[e] = first
        wide = first.astype(jnp.float32)
        first_slopes[e] = 1.0 - wide * wide
        second = jnp.tanh(contract(w_mid[...], first, 0, 0) + bias_mid).astype(jnp.bfloat16)
        seconds[e] = second
        wide = second.astype(jnp.float32)
        second_slopes[e] = 1.0 - wide * wide
        return carry

    lax.fori_loop(0, ELEMS, forward, 0)

    pl.semaphore_wait(far_one, 2)
    for d in (6, -6):
        signal(far_two, along_z(d))

    def arrived(h, blocks, top, bottom):
        where_block = inv_block[h]
        where_lane = inv_lane[h]
        for b in blocks:
            match = where_block == b + 1
            if b < FACE_BLOCKS:
                upper, lower = face_in[b, 0:8], face_in[b, 8:16]
            else:
                k = 2 * (b - FACE_BLOCKS)
                upper = jnp.where(leading, diag_in[k + 1, 0:8], diag_in[k, 0:8])
                lower = jnp.where(leading, diag_in[k + 1, 8:16], diag_in[k, 8:16])
            top = jnp.where(match, pick(upper, where_lane), top)
            bottom = jnp.where(match, pick(lower, where_lane), bottom)
        return top, bottom

    def assemble_some(h, carry):
        zero = jnp.zeros((8, LANES), jnp.float32)
        top, bottom = arrived(h, (0, 1, 2, 3, 4, 5, 12, 13), zero, zero)
        asm[0:8, span(h, LANES)] = top
        asm[8:16, span(h, LANES)] = bottom
        return carry

    def assemble(h, carry):
        top, bottom = asm[0:8, span(h, LANES)], asm[8:16, span(h, LANES)]
        top, bottom = arrived(h, range(6, 12), top, bottom)
        shared = inv_block[h] > 0
        own = cot16[0:8, span(h, LANES)]
        asm[0:8, span(h, LANES)] = jnp.where(shared, 0.5 * own + 0.5 * top, own)
        own = cot16[8:16, span(h, LANES)]
        asm[8:16, span(h, LANES)] = jnp.where(shared, 0.5 * own + 0.5 * bottom, own)
        return carry

    for copy in halo[2:]:
        copy.wait_recv()
    lax.fori_loop(0, CHUNKS, assemble_some, 0, unroll=2)
    for copy in halo[:2]:
        copy.wait_recv()
    lax.fori_loop(0, CHUNKS, assemble, 0, unroll=4)
    pl.semaphore_wait(far_two, 2)
    for d in (4, -4):
        signal(far_three, along_z(d))

    grads[...] = jnp.zeros_like(grads)

    def backward(e, carry):
        here = span(e, NODES)
        impulse = (step_scale * asm[0:FIELDS, here]).astype(jnp.bfloat16)
        first, second = firsts[e], seconds[e]
        back_second = contract(w_out[...], impulse, 0, 0) * second_slopes[e]
        back_second = back_second.astype(jnp.bfloat16)
        back_first = contract(w_mid[...], back_second, 1, 0) * first_slopes[e]
        back_first = back_first.astype(jnp.bfloat16)
        back_firsts[e] = back_first
        grads[0:128] += contract(first, back_second, 1, 1)
        grads[128 : 128 + FIELDS] += contract(state[:, here], back_first, 1, 1)
        grads[144 : 144 + FIELDS] += contract(impulse, second, 1, 1)
        return carry

    lax.fori_loop(0, ELEMS, backward, 0)

    for r in range(32):
        pieces[r] = grads[PIECE * r : PIECE * (r + 1)]
    pl.semaphore_wait(plane_here, 3)
    arriving = [
        push(pieces.at[step_rank(step)], plane_in.at[i], rs_send.at[i], rs_recv.at[i], in_plane(step))
        for i, step in enumerate(PLANE)
    ]
    total = pieces[rank]
    for i, copy in enumerate(arriving):
        copy.wait_recv()
        total = total + plane_in[i]

    along[z] = total
    pl.semaphore_wait(far_three, 2)
    across_z = [
        push(along.at[z], along.at[z], z_send.at[d - 1], z_recv.at[d - 1], along_z(d))
        for d in sorted(range(1, DEPTH), key=lambda d: (-min(d, DEPTH - d), d))
    ]

    for fetch in fetches[8:]:
        fetch.wait()
    rows = jnp.concatenate([asm[:, e * NODES : (e + 1) * NODES] for e in range(ELEMS)], axis=0)
    high = rows.astype(jnp.bfloat16)
    low = (rows - high.astype(jnp.float32)).astype(jnp.bfloat16)
    along_one = (
        contract(high, one[0], 1, 0) + contract(low, one[0], 1, 0) + contract(high, one[1], 1, 0)
    )
    for e in range(ELEMS):
        toward = contract(w_in[...], back_firsts[e], 1, 0)
        for part in range(NODES // LANES):
            lanes = slice(part * LANES, (part + 1) * LANES)
            high_here = high[e * ROWS : (e + 1) * ROWS, lanes]
            low_here = low[e * ROWS : (e + 1) * ROWS, lanes]
            others = (
                contract(high_here, two_three[0], 1, 0)
                + contract(low_here, two_three[0], 1, 0)
                + contract(high_here, two_three[1], 1, 0)
            )
            viscous = -(
                diff[0, e] * along_one[e * ROWS : (e + 1) * ROWS, lanes]
                + diff[1, e] * others[:, 0:LANES]
                + diff[2, e] * others[:, LANES:]
            )
            chunk = e * (NODES // LANES) + part
            value = asm[:, chunk * LANES : (chunk + 1) * LANES] + step_scale * viscous
            out[pl.ds(chunk, FIELDS, stride=CHUNKS), :] = value[0:FIELDS] + toward[:, lanes]

    for copy in sends:
        copy.wait_send()
    sends.clear()
    for copy in reversed(across_z):
        copy.wait_recv()
    total = along[0]
    for d in range(1, DEPTH):
        total = total + along[d]

    final[rank] = total
    arriving = [
        push(final.at[rank], final.at[rank], g_send.at[i], g_recv.at[i], in_plane(step))
        for i, step in enumerate(PLANE)
    ]
    for copy in arriving:
        copy.wait_recv()
    for copy in sends:
        copy.wait_send()


def finish(state_in, final, state_out, gin, gmid, gout, rows, sem):
    copy = pltpu.make_async_copy(state_in, state_out, sem)
    copy.start()
    for r in range(32):
        rows[PIECE * r : PIECE * (r + 1)] = final[r]
    gmid[...] = rows[0:128]
    gin[...] = rows[128 : 128 + FIELDS]
    gout[...] = rows[144 : 144 + FIELDS]
    copy.wait()


def per_device(state, cotangent, diffusivity, shared_nodes, w_in, b_in, w_mid, b_mid, w_out):
    f32, bf16 = jnp.float32, jnp.bfloat16
    one, two_three = direction_tables()
    vmem = pl.BlockSpec(memory_space=pltpu.VMEM)
    hbm = pl.BlockSpec(memory_space=pltpu.HBM)
    dma = pltpu.SemaphoreType.DMA
    result, final = pl.pallas_call(
        body,
        out_shape=(
            pltpu.VMEM((FIELDS * CHUNKS, LANES), f32),
            pltpu.VMEM((32, PIECE, LANES), f32),
        ),
        in_specs=[hbm] * 11,
        out_specs=(vmem, vmem),
        scratch_shapes=[
            pltpu.VMEM((FIELDS, LOCAL), bf16),
            pltpu.VMEM((FIELDS * CHUNKS, LANES), f32),
            pltpu.SMEM((3, ELEMS), f32),
            pltpu.VMEM((1, 8, SLOTS), jnp.int32),
            pltpu.VMEM((FIELDS, HIDDEN), bf16),
            pltpu.VMEM((HIDDEN,), f32),
            pltpu.VMEM((HIDDEN, HIDDEN), bf16),
            pltpu.VMEM((HIDDEN,), f32),
            pltpu.VMEM((FIELDS, HIDDEN), bf16),
            pltpu.VMEM((2, NODES, NODES), bf16),
            pltpu.VMEM((2, LANES, 2 * LANES), bf16),
            pltpu.VMEM((ROWS, LOCAL), f32),
            pltpu.VMEM((BLOCKS, 8, LANES), jnp.int32),
            pltpu.VMEM((BLOCKS, ROWS, LANES), f32),
            pltpu.VMEM((FACE_BLOCKS, ROWS, LANES), f32),
            pltpu.VMEM((4, ROWS, LANES), f32),
            pltpu.VMEM((64, BLOCKS * LANES), bf16),
            pltpu.VMEM((LANES, BLOCKS * LANES), bf16),
            pltpu.VMEM((CHUNKS, 8, LANES), jnp.int32),
            pltpu.VMEM((CHUNKS, 8, LANES), jnp.int32),
            pltpu.VMEM((ROWS, LOCAL), f32),
            pltpu.VMEM((ELEMS, HIDDEN, NODES), bf16),
            pltpu.VMEM((ELEMS, HIDDEN, NODES), bf16),
            pltpu.VMEM((ELEMS, HIDDEN, NODES), f32),
            pltpu.VMEM((ELEMS, HIDDEN, NODES), f32),
            pltpu.VMEM((ELEMS, HIDDEN, NODES), bf16),
            pltpu.VMEM((160, HIDDEN), f32),
            pltpu.VMEM((32, PIECE, LANES), f32),
            pltpu.VMEM((31, PIECE, LANES), f32),
            pltpu.VMEM((DEPTH, PIECE, LANES), f32),
            dma((11,)),
            dma((8,)),
            dma((8,)),
            dma((31,)),
            dma((31,)),
            dma((DEPTH - 1,)),
            dma((DEPTH - 1,)),
            dma((31,)),
            dma((31,)),
            pltpu.SemaphoreType.REGULAR,
            pltpu.SemaphoreType.REGULAR,
            pltpu.SemaphoreType.REGULAR,
            pltpu.SemaphoreType.REGULAR,
        ],
        compiler_params=pltpu.CompilerParams(
            collective_id=0, has_side_effects=True, vmem_limit_bytes=66_500_000
        ),
    )(
        state,
        cotangent.reshape(FIELDS * CHUNKS, LANES),
        diffusivity,
        shared_nodes,
        w_in,
        b_in,
        w_mid,
        b_mid,
        w_out.T,
        jnp.asarray(one),
        jnp.asarray(two_three),
    )
    grad_state, grad_in, grad_mid, grad_out = pl.pallas_call(
        finish,
        out_shape=(
            jax.ShapeDtypeStruct((FIELDS * CHUNKS, LANES), f32),
            jax.ShapeDtypeStruct((FIELDS, HIDDEN), f32),
            jax.ShapeDtypeStruct((HIDDEN, HIDDEN), f32),
            jax.ShapeDtypeStruct((FIELDS, HIDDEN), f32),
        ),
        in_specs=[vmem, vmem],
        out_specs=(hbm, vmem, vmem, vmem),
        scratch_shapes=[pltpu.VMEM((160, HIDDEN), f32), dma],
        compiler_params=pltpu.CompilerParams(vmem_limit_bytes=8 * 1024 * 1024),
    )(result, final)
    return grad_state.reshape(1, FIELDS, LOCAL), grad_in, grad_mid, grad_out.T


def solution(mesh):
    in_specs = (
        P(None, "graph"),
        P("group", None, "graph"),
        P(None, "graph"),
        P("graph", None, None),
        P(),
        P(),
        P(),
        P(),
        P(),
    )
    out_specs = (P("group", None, "graph"), P(), P(), P())
    return jax.shard_map(
        per_device, mesh=mesh, in_specs=in_specs, out_specs=out_specs, check_vma=False
    )
```

```python
import jax
import jax.numpy as jnp
import numpy as np
import ml_dtypes
from jax import lax
from jax.experimental import pallas as pl
from jax.experimental.pallas import tpu as pltpu
from jax.sharding import PartitionSpec as P

FIELDS = 14
ROWS = 16
HIDDEN = 128
NODES = 512
ELEMS = 8
LANES = 128
LOCAL = ELEMS * NODES
CHUNKS = LOCAL // LANES
PROWS = 4
SLOTS = 384
FACE_BLOCKS = 12
BLOCKS = 14
PIECE = 5
MESH = pl.DeviceIdType.MESH
OFFSETS = (1, -1, PROWS, -PROWS, PROWS + 1, -PROWS - 1, PROWS - 1, -PROWS + 1)
PLANE = sorted(
    ((dx, dy, dc) for dx in range(4) for dy in range(4) for dc in range(2) if dx or dy or dc),
    key=lambda step: -min(step[0], 4 - step[0]) - min(step[1], 4 - step[1]),
)
DEPTH = 32
NEAR_Z = (4, -4, 3, -3, 2, -2, 1, -1)

step_scale = 0.5


def stiffness_table():
    order = 7
    points = np.cos(np.pi * np.arange(order + 1) / order)
    ends = np.ones(order + 1)
    ends[0] = 2.0
    ends[-1] = 2.0
    deriv = np.zeros((order + 1, order + 1))
    for first in range(order + 1):
        for second in range(order + 1):
            if first != second:
                deriv[first, second] = (
                    ends[first]
                    / ends[second]
                    * (-1.0) ** (first + second)
                    / (points[first] - points[second])
                )
    row_sums = deriv.sum(axis=1)
    for place in range(order + 1):
        deriv[place, place] = -row_sums[place]
    return deriv.T @ deriv


def split_table(table):
    high = table.astype(ml_dtypes.bfloat16)
    low = (table - high.astype(np.float64)).astype(ml_dtypes.bfloat16)
    return np.stack([high, low])


def direction_tables():
    table = stiffness_table()
    along_one = np.kron(table, np.eye(64)).T
    along_two = np.kron(np.eye(2), np.kron(table, np.eye(8))).T
    along_three = np.kron(np.eye(16), table).T
    return split_table(along_one), split_table(np.concatenate([along_two, along_three], axis=1))


def pick(block, places):
    return jnp.take_along_axis(block, places, axis=1, mode="promise_in_bounds")


def contract(left, right, left_dim, right_dim):
    return lax.dot_general(
        left,
        right,
        (((left_dim,), (right_dim,)), ((), ())),
        preferred_element_type=jnp.float32,
    )


def span(which, size):
    return pl.ds(pl.multiple_of(which * size, size), size)


def body(
    state_hbm,
    cot_hbm,
    diff_hbm,
    lists_hbm,
    w_in_hbm,
    b_in_hbm,
    w_mid_hbm,
    b_mid_hbm,
    w_out_hbm,
    one_hbm,
    two_three_hbm,
    out,
    final,
    state,
    cot,
    diff,
    lists,
    w_in,
    b_in,
    w_mid,
    b_mid,
    w_out,
    one,
    two_three,
    cot16,
    send_idx,
    send_blocks,
    face_in,
    diag_in,
    slot_high,
    slot_low,
    inv_block,
    inv_lane,
    asm,
    firsts,
    seconds,
    first_slopes,
    second_slopes,
    back_firsts,
    grads,
    pieces,
    plane_in,
    along,
    fetched,
    halo_send,
    halo_recv,
    rs_send,
    rs_recv,
    z_send,
    z_recv,
    g_send,
    g_recv,
    far_one,
    far_two,
):
    graph = lax.axis_index("graph")
    x = lax.axis_index("group")
    z = lax.div(graph, 8)
    q = lax.rem(graph, 8)
    y = lax.div(q, 2)
    core = lax.rem(q, 2)
    rank = x * 8 + q

    def place(z_at, q_at, x_at):
        return {"graph": z_at * 8 + q_at, "group": x_at}

    def beside(offset):
        return {"graph": lax.rem(graph + (offset + 256), 256), "group": x}

    def step_place(step):
        dx, dy, dc = step
        q_at = lax.rem(y + dy, 4) * 2 + lax.rem(core + dc, 2)
        return q_at, lax.rem(x + dx, 4)

    def step_rank(step):
        q_at, x_at = step_place(step)
        return x_at * 8 + q_at

    def in_plane(step):
        return place(z, *step_place(step))

    def along_z(d):
        return place(lax.rem(z + (d + 32), 32), q, x)

    def signal(semaphore, target):
        pl.semaphore_signal(semaphore, inc=1, device_id=target, device_id_type=MESH)

    fetches = [
        pltpu.make_async_copy(source, target, fetched.at[i])
        for i, (source, target) in enumerate(
            (
                (cot_hbm, cot),
                (lists_hbm, lists),
                (state_hbm, state),
                (w_in_hbm, w_in),
                (b_in_hbm, b_in),
                (w_mid_hbm, w_mid),
                (b_mid_hbm, b_mid),
                (w_out_hbm, w_out),
                (diff_hbm, diff),
                (one_hbm, one),
                (two_three_hbm, two_three),
            )
        )
    ]
    for fetch in fetches:
        fetch.start()

    barrier = pltpu.get_barrier_semaphore()
    near = [along_z(d) for d in NEAR_Z]
    near += [beside(o) for o in OFFSETS]
    near += [in_plane(step) for step in PLANE]
    for target in near:
        signal(barrier, target)

    fetches[0].wait()
    for h in range(CHUNKS):
        cot16[0:FIELDS, h * LANES : (h + 1) * LANES] = cot[pl.ds(h, FIELDS, stride=CHUNKS), :]
    cot16[FIELDS:ROWS, :] = jnp.zeros((ROWS - FIELDS, LOCAL), jnp.float32)
    fetches[1].wait()
    lane = lax.broadcasted_iota(jnp.int32, (1, LANES), 1)
    leading = lane < 64

    def list_row(which, block):
        return lists[0, which : which + 1, block * LANES : (block + 1) * LANES]

    sent, received = [], []
    for b in range(FACE_BLOCKS):
        row = list_row(b // 3, b % 3)
        sent.append(row)
        received.append(row)
    for k in (4, 6):
        low, high = list_row(k, 0), list_row(k + 1, 0)
        sent.append(jnp.where(leading, low, pltpu.roll(high, 64, 1)))
        received.append(jnp.where(leading, high, pltpu.roll(low, 64, 1)))
    for b in range(BLOCKS):
        send_idx[b] = jnp.broadcast_to(sent[b], (8, LANES))

    def gather_block(b, carry):
        idx = send_idx[b]
        low = jnp.bitwise_and(idx, LANES - 1)
        high = jnp.right_shift(idx, 7)
        top = jnp.zeros((8, LANES), jnp.float32)
        bottom = jnp.zeros((8, LANES), jnp.float32)
        for h in range(CHUNKS):
            match = high == h
            lanes = slice(h * LANES, (h + 1) * LANES)
            top = jnp.where(match, pick(cot16[0:8, lanes], low), top)
            bottom = jnp.where(match, pick(cot16[8:16, lanes], low), bottom)
        send_blocks[b, 0:8] = top
        send_blocks[b, 8:16] = bottom
        return carry

    lax.fori_loop(0, BLOCKS, gather_block, 0, unroll=2)

    sends = []

    def push(source, target, send_sem, recv_sem, device):
        copy = pltpu.make_async_remote_copy(
            src_ref=source,
            dst_ref=target,
            send_sem=send_sem,
            recv_sem=recv_sem,
            device_id=device,
            device_id_type=MESH,
        )
        copy.start()
        sends.append(copy)
        return copy

    pl.semaphore_wait(barrier, len(near))
    halo = []
    for k in (2, 3, 0, 1, 4, 5, 6, 7):
        if k < 4:
            source = send_blocks.at[3 * k : 3 * k + 3, 0:FIELDS]
            target = face_in.at[3 * (k ^ 1) : 3 * (k ^ 1) + 3, 0:FIELDS]
        else:
            source = send_blocks.at[FACE_BLOCKS + (k - 4) // 2, 0:FIELDS]
            target = diag_in.at[(k ^ 1) - 4, 0:FIELDS]
        halo.append(push(source, target, halo_send.at[k], halo_recv.at[k ^ 1], beside(OFFSETS[k])))
    for d in (4, -4):
        signal(far_one, along_z(d))

    lane_f = lane.astype(jnp.float32)
    rows32 = lax.broadcasted_iota(jnp.int32, (CHUNKS, LANES), 0)
    rows128 = lax.broadcasted_iota(jnp.int32, (LANES, LANES), 0)
    for b in range(BLOCKS):
        low = jnp.bitwise_and(received[b], LANES - 1)
        high = jnp.right_shift(received[b], 7)
        match = rows32 == high
        lanes = slice(b * LANES, (b + 1) * LANES)
        slot_high[0:32, lanes] = jnp.where(match, float(b + 1), 0.0).astype(jnp.bfloat16)
        slot_high[32:64, lanes] = jnp.where(match, lane_f, 0.0).astype(jnp.bfloat16)
        slot_low[:, lanes] = jnp.where(rows128 == low, 1.0, 0.0).astype(jnp.bfloat16)
    inverse = contract(slot_high[...], slot_low[...], 1, 1).astype(jnp.int32)
    for h in range(CHUNKS):
        inv_block[h] = jnp.broadcast_to(inverse[h : h + 1], (8, LANES))
        inv_lane[h] = jnp.broadcast_to(inverse[32 + h : 33 + h], (8, LANES))

    for fetch in fetches[2:8]:
        fetch.wait()
    bias_in = jnp.broadcast_to(b_in[...].reshape(1, HIDDEN), (HIDDEN, HIDDEN)).T[:, 0:1]
    bias_mid = jnp.broadcast_to(b_mid[...].reshape(1, HIDDEN), (HIDDEN, HIDDEN)).T[:, 0:1]

    def forward(e, carry):
        inputs = state[:, span(e, NODES)]
        first = jnp.tanh(contract(w_in[...], inputs, 0, 0) + bias_in).astype(jnp.bfloat16)
        firsts[e] = first
        wide = first.astype(jnp.float32)
        first_slopes[e] = 1.0 - wide * wide
        second = jnp.tanh(contract(w_mid[...], first, 0, 0) + bias_mid).astype(jnp.bfloat16)
        seconds[e] = second
        wide = second.astype(jnp.float32)
        second_slopes[e] = 1.0 - wide * wide
        return carry

    lax.fori_loop(0, ELEMS, forward, 0)

    pl.semaphore_wait(far_one, 2)
    for d in (8, -8):
        signal(far_two, along_z(d))

    def arrived(h, blocks, top, bottom):
        where_block = inv_block[h]
        where_lane = inv_lane[h]
        for b in blocks:
            match = where_block == b + 1
            if b < FACE_BLOCKS:
                upper, lower = face_in[b, 0:8], face_in[b, 8:16]
            else:
                k = 2 * (b - FACE_BLOCKS)
                upper = jnp.where(leading, diag_in[k + 1, 0:8], diag_in[k, 0:8])
                lower = jnp.where(leading, diag_in[k + 1, 8:16], diag_in[k, 8:16])
            top = jnp.where(match, pick(upper, where_lane), top)
            bottom = jnp.where(match, pick(lower, where_lane), bottom)
        return top, bottom

    def assemble(h, carry):
        zero = jnp.zeros((8, LANES), jnp.float32)
        top, bottom = arrived(h, range(BLOCKS), zero, zero)
        shared = inv_block[h] > 0
        own = cot16[0:8, span(h, LANES)]
        asm[0:8, span(h, LANES)] = jnp.where(shared, 0.5 * own + 0.5 * top, own)
        own = cot16[8:16, span(h, LANES)]
        asm[8:16, span(h, LANES)] = jnp.where(shared, 0.5 * own + 0.5 * bottom, own)
        return carry

    for copy in halo:
        copy.wait_recv()
    grads[...] = jnp.zeros_like(grads)

    def assemble_element(e):
        for part in range(NODES // LANES):
            assemble(e * (NODES // LANES) + part, 0)

    def backward(e, ahead):
        here = span(e, NODES)
        impulse = (step_scale * asm[0:FIELDS, here]).astype(jnp.bfloat16)
        if ahead:
            assemble_element(e + 1)
        first, second = firsts[e], seconds[e]
        back_second = contract(w_out[...], impulse, 0, 0) * second_slopes[e]
        back_second = back_second.astype(jnp.bfloat16)
        back_first = contract(w_mid[...], back_second, 1, 0) * first_slopes[e]
        back_first = back_first.astype(jnp.bfloat16)
        back_firsts[e] = back_first
        grads[0:128] += contract(first, back_second, 1, 1)
        grads[128 : 128 + FIELDS] += contract(state[:, here], back_first, 1, 1)
        grads[144 : 144 + FIELDS] += contract(impulse, second, 1, 1)

    def backward_ahead(e, carry):
        backward(e, True)
        return carry

    assemble_element(0)
    lax.fori_loop(0, ELEMS - 1, backward_ahead, 0)
    backward(ELEMS - 1, False)

    for r in range(32):
        pieces[r] = grads[PIECE * r : PIECE * (r + 1)]
    arriving = [
        push(pieces.at[step_rank(step)], plane_in.at[i], rs_send.at[i], rs_recv.at[i], in_plane(step))
        for i, step in enumerate(PLANE)
    ]
    total = pieces[rank]
    for i, copy in enumerate(arriving):
        copy.wait_recv()
        total = total + plane_in[i]

    along[z] = total
    pl.semaphore_wait(far_two, 2)
    across_z = [
        push(along.at[z], along.at[z], z_send.at[d - 1], z_recv.at[d - 1], along_z(d))
        for d in sorted(range(1, DEPTH), key=lambda d: (-min(d, DEPTH - d), d))
    ]

    for fetch in fetches[8:]:
        fetch.wait()
    rows = jnp.concatenate([asm[:, e * NODES : (e + 1) * NODES] for e in range(ELEMS)], axis=0)
    high = rows.astype(jnp.bfloat16)
    low = (rows - high.astype(jnp.float32)).astype(jnp.bfloat16)
    along_one = (
        contract(high, one[0], 1, 0) + contract(low, one[0], 1, 0) + contract(high, one[1], 1, 0)
    )
    for e in range(ELEMS):
        toward = contract(w_in[...], back_firsts[e], 1, 0)
        for part in range(NODES // LANES):
            lanes = slice(part * LANES, (part + 1) * LANES)
            high_here = high[e * ROWS : (e + 1) * ROWS, lanes]
            low_here = low[e * ROWS : (e + 1) * ROWS, lanes]
            others = (
                contract(high_here, two_three[0], 1, 0)
                + contract(low_here, two_three[0], 1, 0)
                + contract(high_here, two_three[1], 1, 0)
            )
            viscous = -(
                diff[0, e] * along_one[e * ROWS : (e + 1) * ROWS, lanes]
                + diff[1, e] * others[:, 0:LANES]
                + diff[2, e] * others[:, LANES:]
            )
            chunk = e * (NODES // LANES) + part
            value = asm[:, chunk * LANES : (chunk + 1) * LANES] + step_scale * viscous
            out[pl.ds(chunk, FIELDS, stride=CHUNKS), :] = value[0:FIELDS] + toward[:, lanes]

    for copy in sends:
        copy.wait_send()
    sends.clear()
    for copy in reversed(across_z):
        copy.wait_recv()
    total = along[0]
    for d in range(1, DEPTH):
        total = total + along[d]

    final[rank] = total
    arriving = [
        push(final.at[rank], final.at[rank], g_send.at[i], g_recv.at[i], in_plane(step))
        for i, step in enumerate(PLANE)
    ]
    for copy in arriving:
        copy.wait_recv()
    for copy in sends:
        copy.wait_send()


def finish(state_in, final, state_out, gin, gmid, gout, rows, sem):
    copy = pltpu.make_async_copy(state_in, state_out, sem)
    copy.start()
    for r in range(32):
        rows[PIECE * r : PIECE * (r + 1)] = final[r]
    gmid[...] = rows[0:128]
    gin[...] = rows[128 : 128 + FIELDS]
    gout[...] = rows[144 : 144 + FIELDS]
    copy.wait()


def per_device(state, cotangent, diffusivity, shared_nodes, w_in, b_in, w_mid, b_mid, w_out):
    f32, bf16 = jnp.float32, jnp.bfloat16
    one, two_three = direction_tables()
    vmem = pl.BlockSpec(memory_space=pltpu.VMEM)
    hbm = pl.BlockSpec(memory_space=pltpu.HBM)
    dma = pltpu.SemaphoreType.DMA
    result, final = pl.pallas_call(
        body,
        out_shape=(
            pltpu.VMEM((FIELDS * CHUNKS, LANES), f32),
            pltpu.VMEM((32, PIECE, LANES), f32),
        ),
        in_specs=[hbm] * 11,
        out_specs=(vmem, vmem),
        scratch_shapes=[
            pltpu.VMEM((FIELDS, LOCAL), bf16),
            pltpu.VMEM((FIELDS * CHUNKS, LANES), f32),
            pltpu.SMEM((3, ELEMS), f32),
            pltpu.VMEM((1, 8, SLOTS), jnp.int32),
            pltpu.VMEM((FIELDS, HIDDEN), bf16),
            pltpu.VMEM((HIDDEN,), f32),
            pltpu.VMEM((HIDDEN, HIDDEN), bf16),
            pltpu.VMEM((HIDDEN,), f32),
            pltpu.VMEM((FIELDS, HIDDEN), bf16),
            pltpu.VMEM((2, NODES, NODES), bf16),
            pltpu.VMEM((2, LANES, 2 * LANES), bf16),
            pltpu.VMEM((ROWS, LOCAL), f32),
            pltpu.VMEM((BLOCKS, 8, LANES), jnp.int32),
            pltpu.VMEM((BLOCKS, ROWS, LANES), f32),
            pltpu.VMEM((FACE_BLOCKS, ROWS, LANES), f32),
            pltpu.VMEM((4, ROWS, LANES), f32),
            pltpu.VMEM((64, BLOCKS * LANES), bf16),
            pltpu.VMEM((LANES, BLOCKS * LANES), bf16),
            pltpu.VMEM((CHUNKS, 8, LANES), jnp.int32),
            pltpu.VMEM((CHUNKS, 8, LANES), jnp.int32),
            pltpu.VMEM((ROWS, LOCAL), f32),
            pltpu.VMEM((ELEMS, HIDDEN, NODES), bf16),
            pltpu.VMEM((ELEMS, HIDDEN, NODES), bf16),
            pltpu.VMEM((ELEMS, HIDDEN, NODES), f32),
            pltpu.VMEM((ELEMS, HIDDEN, NODES), f32),
            pltpu.VMEM((ELEMS, HIDDEN, NODES), bf16),
            pltpu.VMEM((160, HIDDEN), f32),
            pltpu.VMEM((32, PIECE, LANES), f32),
            pltpu.VMEM((31, PIECE, LANES), f32),
            pltpu.VMEM((DEPTH, PIECE, LANES), f32),
            dma((11,)),
            dma((8,)),
            dma((8,)),
            dma((31,)),
            dma((31,)),
            dma((DEPTH - 1,)),
            dma((DEPTH - 1,)),
            dma((31,)),
            dma((31,)),
            pltpu.SemaphoreType.REGULAR,
            pltpu.SemaphoreType.REGULAR,
        ],
        compiler_params=pltpu.CompilerParams(
            collective_id=0, has_side_effects=True, vmem_limit_bytes=66_500_000
        ),
    )(
        state,
        cotangent.reshape(FIELDS * CHUNKS, LANES),
        diffusivity,
        shared_nodes,
        w_in,
        b_in,
        w_mid,
        b_mid,
        w_out.T,
        jnp.asarray(one),
        jnp.asarray(two_three),
    )
    grad_state, grad_in, grad_mid, grad_out = pl.pallas_call(
        finish,
        out_shape=(
            jax.ShapeDtypeStruct((FIELDS * CHUNKS, LANES), f32),
            jax.ShapeDtypeStruct((FIELDS, HIDDEN), f32),
            jax.ShapeDtypeStruct((HIDDEN, HIDDEN), f32),
            jax.ShapeDtypeStruct((FIELDS, HIDDEN), f32),
        ),
        in_specs=[vmem, vmem],
        out_specs=(hbm, vmem, vmem, vmem),
        scratch_shapes=[pltpu.VMEM((160, HIDDEN), f32), dma],
        compiler_params=pltpu.CompilerParams(vmem_limit_bytes=8 * 1024 * 1024),
    )(result, final)
    return grad_state.reshape(1, FIELDS, LOCAL), grad_in, grad_mid, grad_out.T


def solution(mesh):
    in_specs = (
        P(None, "graph"),
        P("group", None, "graph"),
        P(None, "graph"),
        P("graph", None, None),
        P(),
        P(),
        P(),
        P(),
        P(),
    )
    out_specs = (P("group", None, "graph"), P(), P(), P())
    return jax.shard_map(
        per_device, mesh=mesh, in_specs=in_specs, out_specs=out_specs, check_vma=False
    )
```
